32 devices in a mesh: dp: 8 (over z, y), mp: 4 (over x, core).
Axes of the slice: x: 2, y: 2, z: 4, core: 2. Of those that a mesh axis runs over, the one named last changes fastest.
Arguments:
- ids: int32 [8192], P('dp'), may hold values from 0 to 16777215, as said below
- hash_a: int32 [1024], replicated, may hold values from 1 to 16383
- hash_b: int32 [1024], replicated, may hold values from 0 to 16383
- hash_p: int32 [1024], replicated, may hold values from 16384 to 32767
- hash_m: int32 [1024], replicated, may hold values from 4096 to 16383
- w_in: bfloat16 [1024, 2048], P(None, 'mp'), may hold values from -0.1875 to 0.1875
- w_mid: bfloat16 [2, 2048, 2048], P(None, None, 'mp'), may hold values from -0.125 to 0.125
- w_out: bfloat16 [2048, 64], P('mp'), may hold values from -0.125 to 0.125
- bn_gain: float32 [3, 2048], P(None, 'mp'), may hold values from 0.25 to 1.75
- bn_bias: float32 [3, 2048], P(None, 'mp'), may hold values from -3 to 3
- target: float32 [8192, 64], P('dp'), may hold values from -6 to 6
Outputs:
- grad_w_in: float32 [1024, 2048], P('dp', 'mp')
- grad_w_mid: float32 [2, 2048, 2048], P(None, 'dp', 'mp')
- grad_w_out: float32 [2048, 64], P(('mp', 'dp'))
- grad_gain: float32 [3, 2048], P(None, 'mp')
- grad_bias: float32 [3, 2048], P(None, 'mp')
The draws below stay inside these ranges and needn't reach their ends.
Inputs may be any that keep to these rules, and one draw needn't show every extreme that they name: The number of distinct ids among one device's 1024 rows differs from device to device, from one to many.
All inputs are finite; a program needn't handle non-finite values.
Results may differ from the reference program's by a relative error of at most 0.02.
Values may be sent and summed in bfloat16 or wider, within the bound.
A program may use at most 128 MiB of HBM per device.

```python
import math
import jax
import jax.numpy as jnp
from jax import lax

K = 1024
HID = 2048
OUT = 64
LAYERS = 3
ROWS_DEV = 1024
BATCH = 8192


def draw_ids(key, part):
    level_key = jax.random.fold_in(key, 11)
    pool_key = jax.random.fold_in(key, 12)
    pick_key = jax.random.fold_in(key, 13)
    blocks = BATCH // ROWS_DEV
    levels = jax.random.randint(level_key, (blocks,), 0, 10)
    distinct = jnp.left_shift(jnp.ones((blocks,), jnp.int32), levels)
    pool = jax.random.randint(pool_key, (blocks, 1024), 0, 16777216)
    picks = jax.random.randint(pick_key, (blocks, ROWS_DEV), 0, 1073741824) % distinct[:, None]
    return jnp.take_along_axis(pool, picks, axis=1).reshape(-1).astype(jnp.int32)


def set_ends(result, rng, smallest, high):
    shape = result.shape
    index_at = [jax.random.randint(jax.random.fold_in(rng, axis), (), 0, shape[axis]) for axis in range(len(shape))]
    result = result.at[tuple(index_at)].set(smallest)
    longest = shape.index(max(shape))
    index_at[longest] = (index_at[longest] + 1) % shape[longest]
    return result.at[tuple(index_at)].set(high)


def shard_levels(rng, shape, pieces, least, high):
    factor_of = 1.0
    for position, blocks in pieces:
        heights = jax.random.uniform(jax.random.fold_in(jax.random.fold_in(rng, 6), position), (blocks,), jnp.float32, least / len(pieces), high / len(pieces))
        factor_of = factor_of * jnp.repeat(jnp.exp(heights), shape[position] // blocks).reshape((-1,) + (1,) * (len(shape) - 1 - position))
    return factor_of


def gaussian(rng, dims, width, bound, split=(), dtype=jnp.bfloat16):
    factor_of = shard_levels(rng, dims, split, -0.22, 0.18) if split else 1.0
    array = jax.random.normal(rng, dims, jnp.float32) * width * factor_of
    return jnp.minimum(jnp.maximum(array, -bound), bound).astype(dtype)


def setup_inputs(seed: int = 0) -> dict:
    splits = jax.random.split(jax.random.key(seed), 12)
    ids = draw_ids(jax.random.fold_in(splits[11], 71), 0)
    hash_a = set_ends(jax.random.randint(splits[1], (K,), 1, 16384), jax.random.fold_in(splits[1], 1), 1, 16383).astype(jnp.int32)
    hash_b = set_ends(jax.random.randint(splits[2], (K,), 0, 16384), jax.random.fold_in(splits[2], 1), 0, 16383).astype(jnp.int32)
    hash_p = set_ends(jax.random.randint(splits[3], (K,), 16384, 32768), jax.random.fold_in(splits[3], 1), 16384, 32767).astype(jnp.int32)
    hash_m = set_ends(jax.random.randint(splits[4], (K,), 4096, 16384), jax.random.fold_in(splits[4], 1), 4096, 16383).astype(jnp.int32)
    w_in = gaussian(splits[5], (K, HID), K ** -0.5, 0.1875, ((1, 4),))
    w_mid = gaussian(splits[6], (LAYERS - 1, HID, HID), HID ** -0.5, 0.125, ((2, 4),))
    w_out = gaussian(splits[7], (HID, OUT), HID ** -0.5, 0.125, ((0, 4),))
    bn_gain = jnp.clip(1.0 + 0.15 * jax.random.normal(splits[8], (LAYERS, HID), jnp.float32), 0.25, 1.75)
    bn_bias = gaussian(splits[9], (LAYERS, HID), 0.5, 3.0, ((1, 4),), jnp.float32)
    target = gaussian(splits[10], (BATCH, OUT), 1.0, 6.0, ((0, 8),), jnp.float32)
    return {"ids": ids, "hash_a": hash_a, "hash_b": hash_b, "hash_p": hash_p, "hash_m": hash_m, "w_in": w_in, "w_mid": w_mid, "w_out": w_out, "bn_gain": bn_gain, "bn_bias": bn_bias, "target": target}


epsilon_norm = 1e-05

def encode(ids, hash_a, hash_b, hash_p, hash_m):
    reduced = ids[:, None] % hash_p[None, :]
    hashed = (hash_a[None, :] * reduced + hash_b[None, :]) % hash_p[None, :] % hash_m[None, :]
    scaled = 2.0 * hashed.astype(jnp.float32) / (hash_m[None, :] - 1).astype(jnp.float32) - 1.0
    return scaled.astype(jnp.bfloat16)

def mish_act(values):
    return values * jnp.tanh(jax.nn.softplus(values))

def mish_slope(values):
    tangent = jnp.tanh(jax.nn.softplus(values))
    return tangent + values * (1.0 - tangent * tangent) * jax.nn.sigmoid(values)

def reference(ids, hash_a, hash_b, hash_p, hash_m, w_in, w_mid, w_out, bn_gain, bn_bias, target):
    inputs = [encode(ids, hash_a, hash_b, hash_p, hash_m)]
    saved = []
    for layer_at in range(LAYERS):
        weights = w_in if layer_at == 0 else w_mid[layer_at - 1]
        summed = jnp.dot(inputs[-1], weights, preferred_element_type=jnp.float32)
        average = lax.optimization_barrier(jnp.mean(summed, axis=0))
        centered = summed - average
        spread = lax.optimization_barrier(jnp.mean(centered * centered, axis=0))
        inverse = 1.0 / jnp.sqrt(spread + epsilon_norm)
        normed = centered * inverse
        shifted = bn_gain[layer_at] * normed + bn_bias[layer_at]
        inputs.append(mish_act(shifted).astype(jnp.bfloat16))
        saved.append((normed, inverse, shifted))
    predicted = jnp.dot(inputs[-1], w_out, preferred_element_type=jnp.float32)
    residual_out = ((predicted - target) / math.sqrt(BATCH)).astype(jnp.bfloat16)
    grad_out = jnp.dot(inputs[-1].T, residual_out, preferred_element_type=jnp.float32)
    upstream = jnp.dot(residual_out, w_out.T, preferred_element_type=jnp.float32)
    grads_gain = []
    grads_bias = []
    grads_weight = []
    for layer_at in reversed(range(LAYERS)):
        normed, inverse, shifted = saved[layer_at]
        slope_a = upstream * mish_slope(shifted)
        bias_sum = lax.optimization_barrier(jnp.sum(slope_a, axis=0))
        gain_sum = lax.optimization_barrier(jnp.sum(slope_a * normed, axis=0))
        slope_z = (bn_gain[layer_at] * inverse * (slope_a - bias_sum / BATCH - normed * gain_sum / BATCH)).astype(jnp.bfloat16)
        grads_weight.append(jnp.dot(inputs[layer_at].T, slope_z, preferred_element_type=jnp.float32))
        if layer_at > 0:
            upstream = jnp.dot(slope_z, w_mid[layer_at - 1].T, preferred_element_type=jnp.float32)
        grads_gain.append(gain_sum)
        grads_bias.append(bias_sum)
    grads_weight = grads_weight[::-1]
    grad_gain = jnp.stack(grads_gain[::-1])
    grad_bias = jnp.stack(grads_bias[::-1])
    return (grads_weight[0], jnp.stack(grads_weight[1:]), grad_out, grad_gain, grad_bias)
```

```python
import functools
import math

import jax
import jax.numpy as jnp
from jax import lax
from jax.experimental import pallas as pl
from jax.experimental.pallas import tpu as pltpu
from jax.sharding import PartitionSpec as P

epsilon_norm = 1e-05


def encode(ids, hash_a, hash_b, hash_p, hash_m):
    p_real = hash_p.astype(jnp.float32)
    m_real = hash_m.astype(jnp.float32)
    p_inv, m_inv, scale = lax.optimization_barrier(
        (1.0 / p_real, 1.0 / m_real, 2.0 / (hash_m - 1).astype(jnp.float32))
    )
    ids_real = ids.astype(jnp.float32)
    guess = (ids_real[:, None] * p_inv[None, :]).astype(jnp.int32)
    reduced = ids[:, None] - guess * hash_p[None, :]
    mixed = hash_a[None, :] * reduced + hash_b[None, :]
    guess = jnp.floor(mixed.astype(jnp.float32) * p_inv[None, :]).astype(jnp.int32)
    rest = (mixed - guess * hash_p[None, :]).astype(jnp.float32)
    rest = jnp.where(rest < 0.0, rest + p_real[None, :], rest)
    rest = jnp.where(rest >= p_real[None, :], rest - p_real[None, :], rest)
    bucket = jnp.floor((rest + 0.5) * m_inv[None, :])
    hashed = rest - bucket * m_real[None, :]
    return (hashed * scale[None, :] - 1.0).astype(jnp.bfloat16)


def exchange_kernel(axis, n, x_ref, o_ref, held, send_sems, recv_sems):
    me = lax.axis_index(axis)
    barrier = pltpu.get_barrier_semaphore()
    for step in range(1, n):
        pl.semaphore_signal(
            barrier,
            inc=1,
            device_id={axis: lax.rem(me + step, n)},
            device_id_type=pl.DeviceIdType.MESH,
        )
    pl.semaphore_wait(barrier, n - 1)
    copies = []
    for step in range(1, n):
        copy = pltpu.make_async_remote_copy(
            src_ref=x_ref,
            dst_ref=held.at[me],
            send_sem=send_sems.at[step],
            recv_sem=recv_sems.at[step],
            device_id={axis: lax.rem(me + step, n)},
            device_id_type=pl.DeviceIdType.MESH,
        )
        copy.start()
        copies.append(copy)
    held[me] = x_ref[...]
    for copy in copies:
        copy.wait()
    total = held[0]
    for at in range(1, n):
        total = total + held[at]
    o_ref[...] = total


def sum_pair(first, second, axis):
    n = lax.axis_size(axis)
    stacked = jnp.stack([first, second]).reshape(8, -1)
    total = pl.pallas_call(
        functools.partial(exchange_kernel, axis, n),
        out_shape=jax.ShapeDtypeStruct(stacked.shape, stacked.dtype),
        in_specs=[pl.BlockSpec(memory_space=pltpu.VMEM)],
        out_specs=pl.BlockSpec(memory_space=pltpu.VMEM),
        scratch_shapes=[
            pltpu.VMEM((n,) + stacked.shape, stacked.dtype),
            pltpu.SemaphoreType.DMA((n,)),
            pltpu.SemaphoreType.DMA((n,)),
        ],
        compiler_params=pltpu.CompilerParams(
            collective_id=0, has_side_effects=True, vmem_limit_bytes=4 << 20
        ),
        name="sum_pair",
    )(stacked).reshape(2, -1)
    return total[0], total[1]


def mish_act(values):
    return values * jnp.tanh(jax.nn.softplus(values))


def mish_slope(values):
    tangent = jnp.tanh(jax.nn.softplus(values))
    return tangent + values * (1.0 - tangent * tangent) * jax.nn.sigmoid(values)


def column_stats(summed, batch_total):
    totals, squares = sum_pair(jnp.sum(summed, axis=0), jnp.sum(summed * summed, axis=0), "dp")
    average = totals / batch_total
    spread = squares / batch_total - average * average
    centered = summed - average
    inverse = 1.0 / jnp.sqrt(spread + epsilon_norm)
    return (centered * inverse, inverse)


def column_products(left_rows, right_rows):
    return jnp.dot(left_rows.T, right_rows, preferred_element_type=jnp.float32)


def per_device(ids, hash_a, hash_b, hash_p, hash_m, w_in, w_mid, w_out, bn_gain, bn_bias, target):
    batch_devices = lax.axis_size("dp")
    batch_total = ids.shape[0] * batch_devices
    layer_count = bn_gain.shape[0]
    encoded = lax.optimization_barrier(encode(ids, hash_a, hash_b, hash_p, hash_m))
    full_inputs = []
    saved = []
    current = encoded
    for layer_at in range(layer_count):
        if layer_at == 0:
            whole_input = encoded
            summed = jnp.dot(whole_input, w_in, preferred_element_type=jnp.float32)
        else:
            whole_input = lax.all_gather(current, "mp", axis=1, tiled=True)
            summed = jnp.dot(whole_input, w_mid[layer_at - 1], preferred_element_type=jnp.float32)
        full_inputs.append(whole_input)
        normed, inverse = column_stats(summed, batch_total)
        shifted = bn_gain[layer_at] * normed + bn_bias[layer_at]
        current = mish_act(shifted).astype(jnp.bfloat16)
        saved.append((normed, inverse, shifted))
    partial_out = jnp.dot(current, w_out, preferred_element_type=jnp.float32)
    predicted = lax.psum(partial_out.astype(jnp.bfloat16), "mp").astype(jnp.float32)
    residual_out = ((predicted - target) / math.sqrt(batch_total)).astype(jnp.bfloat16)
    grad_out = lax.psum_scatter(
        column_products(current, residual_out).astype(jnp.bfloat16),
        "dp",
        scatter_dimension=0,
        tiled=True,
    ).astype(jnp.float32)
    upstream = jnp.dot(residual_out, w_out.T, preferred_element_type=jnp.float32)
    grads_gain = []
    grads_bias = []
    grads_mid = []
    grad_first = None
    for layer_at in reversed(range(layer_count)):
        normed, inverse, shifted = saved[layer_at]
        slope_a = upstream * mish_slope(shifted)
        bias_sum, gain_sum = sum_pair(
            jnp.sum(slope_a, axis=0), jnp.sum(slope_a * normed, axis=0), "dp"
        )
        slope_z = (
            bn_gain[layer_at]
            * inverse
            * (slope_a - bias_sum / batch_total - normed * gain_sum / batch_total)
        ).astype(jnp.bfloat16)
        whole_input = full_inputs[layer_at]
        if layer_at == 0:
            grad_first = lax.psum_scatter(
                column_products(whole_input, slope_z).astype(jnp.bfloat16),
                "dp",
                scatter_dimension=0,
                tiled=True,
            ).astype(jnp.float32)
        else:
            grads_mid.append(
                lax.psum_scatter(
                    column_products(whole_input, slope_z).astype(jnp.bfloat16),
                    "dp",
                    scatter_dimension=0,
                    tiled=True,
                ).astype(jnp.float32)
            )
            weights = w_mid[layer_at - 1]
            partial_in = jnp.dot(slope_z, weights.T, preferred_element_type=jnp.float32)
            upstream = lax.psum_scatter(
                partial_in.astype(jnp.bfloat16), "mp", scatter_dimension=1, tiled=True
            ).astype(jnp.float32)
        grads_gain.append(gain_sum)
        grads_bias.append(bias_sum)
    grad_mid = jnp.stack(grads_mid[::-1])
    grad_gain = jnp.stack(grads_gain[::-1])
    grad_bias = jnp.stack(grads_bias[::-1])
    return (grad_first, grad_mid, grad_out, grad_gain, grad_bias)


def solution(mesh):
    return jax.shard_map(
        per_device,
        mesh=mesh,
        in_specs=(
            P("dp"),
            P(),
            P(),
            P(),
            P(),
            P(None, "mp"),
            P(None, None, "mp"),
            P("mp", None),
            P(None, "mp"),
            P(None, "mp"),
            P("dp", None),
        ),
        out_specs=(
            P("dp", "mp"),
            P(None, "dp", "mp"),
            P(("mp", "dp"), None),
            P(None, "mp"),
            P(None, "mp"),
        ),
        check_vma=False,
    )
```

```python
import functools
import math

import jax
import jax.numpy as jnp
from jax import lax
from jax.experimental import pallas as pl
from jax.experimental.pallas import tpu as pltpu
from jax.sharding import PartitionSpec as P

epsilon_norm = 1e-05


def encode(ids, hash_a, hash_b, hash_p, hash_m):
    p_real = hash_p.astype(jnp.float32)
    m_real = hash_m.astype(jnp.float32)
    p_inv, m_inv, scale = lax.optimization_barrier(
        (1.0 / p_real, 1.0 / m_real, 2.0 / (hash_m - 1).astype(jnp.float32))
    )
    ids_real = ids.astype(jnp.float32)
    guess = (ids_real[:, None] * p_inv[None, :]).astype(jnp.int32)
    reduced = ids[:, None] - guess * hash_p[None, :]
    mixed = hash_a[None, :] * reduced + hash_b[None, :]
    guess = jnp.floor(mixed.astype(jnp.float32) * p_inv[None, :]).astype(jnp.int32)
    rest = (mixed - guess * hash_p[None, :]).astype(jnp.float32)
    rest = jnp.where(rest < 0.0, rest + p_real[None, :], rest)
    rest = jnp.where(rest >= p_real[None, :], rest - p_real[None, :], rest)
    bucket = jnp.floor((rest + 0.5) * m_inv[None, :])
    hashed = rest - bucket * m_real[None, :]
    return (hashed * scale[None, :] - 1.0).astype(jnp.bfloat16)


def exchange_kernel(axis, n, x_ref, o_ref, held, send_sems, recv_sems):
    me = lax.axis_index(axis)
    barrier = pltpu.get_barrier_semaphore()
    for step in range(1, n):
        pl.semaphore_signal(
            barrier,
            inc=1,
            device_id={axis: lax.rem(me + step, n)},
            device_id_type=pl.DeviceIdType.MESH,
        )
    pl.semaphore_wait(barrier, n - 1)
    copies = []
    for step in range(1, n):
        copy = pltpu.make_async_remote_copy(
            src_ref=x_ref,
            dst_ref=held.at[me],
            send_sem=send_sems.at[step],
            recv_sem=recv_sems.at[step],
            device_id={axis: lax.rem(me + step, n)},
            device_id_type=pl.DeviceIdType.MESH,
        )
        copy.start()
        copies.append(copy)
    held[me] = x_ref[...]
    for copy in copies:
        copy.wait()
    total = held[0].astype(jnp.float32)
    for at in range(1, n):
        total = total + held[at].astype(jnp.float32)
    o_ref[...] = total


def exchange_sum(value, axis, collective, name):
    n = lax.axis_size(axis)
    return pl.pallas_call(
        functools.partial(exchange_kernel, axis, n),
        out_shape=jax.ShapeDtypeStruct(value.shape, jnp.float32),
        in_specs=[VMEM_SPEC],
        out_specs=VMEM_SPEC,
        scratch_shapes=[
            pltpu.VMEM((n,) + value.shape, value.dtype),
            pltpu.SemaphoreType.DMA((n,)),
            pltpu.SemaphoreType.DMA((n,)),
        ],
        compiler_params=pltpu.CompilerParams(
            collective_id=collective, has_side_effects=True, vmem_limit_bytes=4 << 20
        ),
        name=name,
    )(value)


def sum_pair(first, second, axis):
    total = exchange_sum(jnp.stack([first, second]).reshape(8, -1), axis, 0, "sum_pair")
    total = total.reshape(2, -1)
    return total[0], total[1]


VMEM_SPEC = pl.BlockSpec(memory_space=pltpu.VMEM)
MESH_ID = pl.DeviceIdType.MESH
CHUNKS = 4


def meet(targets):
    barrier = pltpu.get_barrier_semaphore()
    for target in targets:
        pl.semaphore_signal(barrier, inc=1, device_id=target, device_id_type=MESH_ID)
    pl.semaphore_wait(barrier, len(targets))


def quad_peers(axis):
    me = lax.axis_index(axis)
    near = me + 1 - 2 * lax.rem(me, 2)
    far = lax.rem(me + 2, 4)
    return me, near, far


def gather_kernel(axis, x_ref, o_ref, own_sem, send_sems, recv_sems):
    me, near, far = quad_peers(axis)
    rows, width = x_ref.shape
    part = rows // CHUNKS
    meet([{axis: near}, {axis: far}])

    def place(owner, at):
        return o_ref.at[pl.ds(at * part, part), pl.ds(pl.multiple_of(owner * width, 128), width)]

    def send(source, owner, at, slot, target):
        copy = pltpu.make_async_remote_copy(
            src_ref=source,
            dst_ref=place(owner, at),
            send_sem=send_sems.at[slot, at],
            recv_sem=recv_sems.at[slot, at],
            device_id={axis: target},
            device_id_type=MESH_ID,
        )
        copy.start()
        return copy

    own = []
    far_copies = []
    for at in range(CHUNKS):
        far_copies.append(send(x_ref.at[pl.ds(at * part, part)], me, at, 0, far))
    for at in range(CHUNKS):
        own.append(send(x_ref.at[pl.ds(at * part, part)], me, at, 1, near))
    local = pltpu.make_async_copy(
        x_ref, o_ref.at[:, pl.ds(pl.multiple_of(me * width, 128), width)], own_sem
    )
    local.start()
    for at in range(CHUNKS):
        far_copies[at].wait_recv()
        own.append(send(place(far, at), far, at, 2, near))
    for copy in far_copies:
        copy.wait_send()
    for copy in own:
        copy.wait()
    local.wait()


def gather_columns(value, axis):
    if lax.axis_size(axis) != 4:
        return lax.all_gather(value, axis, axis=1, tiled=True)
    rows, width = value.shape
    return pl.pallas_call(
        functools.partial(gather_kernel, axis),
        out_shape=jax.ShapeDtypeStruct((rows, 4 * width), value.dtype),
        in_specs=[VMEM_SPEC],
        out_specs=VMEM_SPEC,
        scratch_shapes=[
            pltpu.SemaphoreType.DMA,
            pltpu.SemaphoreType.DMA((3, CHUNKS)),
            pltpu.SemaphoreType.DMA((3, CHUNKS)),
        ],
        compiler_params=pltpu.CompilerParams(
            collective_id=2, has_side_effects=True, vmem_limit_bytes=16 << 20
        ),
        name="gather_columns",
    )(value)


def reduce_kernel(axis, n, quad, count, *refs):
    refs = list(refs)
    part_ref = refs.pop(0) if quad else None
    grads = [refs.pop(0) for _ in range(count)]
    up_ref = refs.pop(0) if quad else None
    outs = [refs.pop(0) for _ in range(count)]
    helds = [refs.pop(0) for _ in range(count)]
    send_sems, recv_sems = refs.pop(0), refs.pop(0)
    rank = lax.axis_index(axis)
    peers = [lax.rem(rank + step, n) for step in range(1, n)]
    targets = [{axis: peer} for peer in peers]
    if quad:
        near_buf, sum_buf, far_buf, quad_send, quad_recv = refs
        me, near, far = quad_peers(quad)
        targets = targets + [{quad: near}, {quad: far}]
    meet(targets)
    if quad:
        rows = part_ref.shape[0]
        width = part_ref.shape[1] // 4
        part = rows // CHUNKS

        def columns(owner):
            return pl.ds(pl.multiple_of(owner * width, 128), width)

        near_copies = [[], []]
        for slot, owner in enumerate((lax.rem(near + 2, 4), near)):
            for at in range(CHUNKS):
                copy = pltpu.make_async_remote_copy(
                    src_ref=part_ref.at[pl.ds(at * part, part), columns(owner)],
                    dst_ref=near_buf.at[slot, pl.ds(at * part, part)],
                    send_sem=quad_send.at[slot, at],
                    recv_sem=quad_recv.at[slot, at],
                    device_id={quad: near},
                    device_id_type=MESH_ID,
                )
                copy.start()
                near_copies[slot].append(copy)
    grad_copies = []
    for which in range(count):
        block = outs[which].shape[0]
        for step in range(1, n):
            peer = peers[step - 1]
            copy = pltpu.make_async_remote_copy(
                src_ref=grads[which].at[pl.ds(pl.multiple_of(peer * block, 16), block)],
                dst_ref=helds[which].at[step - 1],
                send_sem=send_sems.at[which, step - 1],
                recv_sem=recv_sems.at[which, step - 1],
                device_id={axis: peer},
                device_id_type=MESH_ID,
            )
            copy.start()
            grad_copies.append(copy)
    if quad:
        stride = 64
        far_copies = []
        for at in range(CHUNKS):
            near_copies[0][at].wait_recv()

            @pl.loop(0, part // stride)
            def _(line):
                here = pl.ds(pl.multiple_of(at * part + line * stride, 16), stride)
                sum_buf[here, :] = (
                    part_ref[here, columns(far)].astype(jnp.float32)
                    + near_buf[0, here, :].astype(jnp.float32)
                ).astype(sum_buf.dtype)

            copy = pltpu.make_async_remote_copy(
                src_ref=sum_buf.at[pl.ds(at * part, part)],
                dst_ref=far_buf.at[pl.ds(at * part, part)],
                send_sem=quad_send.at[2, at],
                recv_sem=quad_recv.at[2, at],
                device_id={quad: far},
                device_id_type=MESH_ID,
            )
            copy.start()
            far_copies.append(copy)
        for at in range(CHUNKS):
            near_copies[1][at].wait_recv()
            far_copies[at].wait_recv()

            @pl.loop(0, part // stride)
            def _(line):
                here = pl.ds(pl.multiple_of(at * part + line * stride, 16), stride)
                up_ref[here, :] = (
                    part_ref[here, columns(me)].astype(jnp.float32)
                    + near_buf[1, here, :].astype(jnp.float32)
                    + far_buf[here, :].astype(jnp.float32)
                )

        for copy in near_copies[0] + near_copies[1] + far_copies:
            copy.wait_send()
    for copy in grad_copies:
        copy.wait()
    for which in range(count):
        block = outs[which].shape[0]
        stride = min(16, block)

        @pl.loop(0, block // stride)
        def _(line):
            here = pl.ds(pl.multiple_of(line * stride, stride), stride)
            mine = pl.ds(pl.multiple_of(rank * block + line * stride, stride), stride)
            total = grads[which][mine, :].astype(jnp.float32)
            for step in range(n - 1):
                total = total + helds[which][step, here, :].astype(jnp.float32)
            outs[which][here, :] = total


def reduce_blocks(partial, grads, collective):
    n = lax.axis_size("dp")
    quad = "mp" if partial is not None else None
    count = len(grads)
    shapes = []
    scratch = []
    operands = []
    if quad:
        rows, width = partial.shape[0], partial.shape[1] // 4
        operands.append(partial)
        shapes.append(jax.ShapeDtypeStruct((rows, width), jnp.float32))
    for grad in grads:
        block = grad.shape[0] // n
        operands.append(grad)
        shapes.append(jax.ShapeDtypeStruct((block, grad.shape[1]), jnp.float32))
        scratch.append(pltpu.VMEM((n - 1, block, grad.shape[1]), grad.dtype))
    scratch += [pltpu.SemaphoreType.DMA((count, n - 1)), pltpu.SemaphoreType.DMA((count, n - 1))]
    if quad:
        scratch += [
            pltpu.VMEM((2, rows, width), partial.dtype),
            pltpu.VMEM((rows, width), partial.dtype),
            pltpu.VMEM((rows, width), partial.dtype),
            pltpu.SemaphoreType.DMA((3, CHUNKS)),
            pltpu.SemaphoreType.DMA((3, CHUNKS)),
        ]
    return pl.pallas_call(
        functools.partial(reduce_kernel, "dp", n, quad, count),
        out_shape=shapes,
        in_specs=[VMEM_SPEC] * len(operands),
        out_specs=[VMEM_SPEC] * len(shapes),
        scratch_shapes=scratch,
        compiler_params=pltpu.CompilerParams(
            collective_id=collective, has_side_effects=True, vmem_limit_bytes=32 << 20
        ),
        name="reduce_blocks",
    )(*operands)


def mish_act(values):
    return values * jnp.tanh(jax.nn.softplus(values))


def mish_slope(values):
    tangent = jnp.tanh(jax.nn.softplus(values))
    return tangent + values * (1.0 - tangent * tangent) * jax.nn.sigmoid(values)


def column_stats(summed, batch_total):
    totals, squares = sum_pair(jnp.sum(summed, axis=0), jnp.sum(summed * summed, axis=0), "dp")
    average = totals / batch_total
    spread = squares / batch_total - average * average
    centered = summed - average
    inverse = 1.0 / jnp.sqrt(spread + epsilon_norm)
    return (centered * inverse, inverse)


def column_products(left_rows, right_rows):
    return jnp.dot(left_rows.T, right_rows, preferred_element_type=jnp.float32)


def per_device(ids, hash_a, hash_b, hash_p, hash_m, w_in, w_mid, w_out, bn_gain, bn_bias, target):
    batch_devices = lax.axis_size("dp")
    batch_total = ids.shape[0] * batch_devices
    layer_count = bn_gain.shape[0]
    encoded = lax.optimization_barrier(encode(ids, hash_a, hash_b, hash_p, hash_m))
    full_inputs = []
    saved = []
    current = encoded
    for layer_at in range(layer_count):
        if layer_at == 0:
            whole_input = encoded
            summed = jnp.dot(whole_input, w_in, preferred_element_type=jnp.float32)
        else:
            whole_input = gather_columns(current, "mp")
            summed = jnp.dot(whole_input, w_mid[layer_at - 1], preferred_element_type=jnp.float32)
        full_inputs.append(whole_input)
        normed, inverse = column_stats(summed, batch_total)
        shifted = bn_gain[layer_at] * normed + bn_bias[layer_at]
        current = mish_act(shifted).astype(jnp.bfloat16)
        saved.append((normed, inverse, shifted))
    partial_out = jnp.dot(current, w_out, preferred_element_type=jnp.float32)
    predicted = exchange_sum(partial_out.astype(jnp.bfloat16), "mp", 1, "sum_output")
    residual_out = ((predicted - target) / math.sqrt(batch_total)).astype(jnp.bfloat16)
    waiting = [column_products(current, residual_out).astype(jnp.bfloat16)]
    grad_out = None
    upstream = jnp.dot(residual_out, w_out.T, preferred_element_type=jnp.float32)
    grads_gain = []
    grads_bias = []
    grads_mid = []
    grad_first = None
    for layer_at in reversed(range(layer_count)):
        normed, inverse, shifted = saved[layer_at]
        slope_a = upstream * mish_slope(shifted)
        bias_sum, gain_sum = sum_pair(
            jnp.sum(slope_a, axis=0), jnp.sum(slope_a * normed, axis=0), "dp"
        )
        slope_z = (
            bn_gain[layer_at]
            * inverse
            * (slope_a - bias_sum / batch_total - normed * gain_sum / batch_total)
        ).astype(jnp.bfloat16)
        whole_input = full_inputs[layer_at]
        waiting = [column_products(whole_input, slope_z).astype(jnp.bfloat16)] + waiting
        partial_in = None
        if layer_at > 0:
            partial_in = jnp.dot(
                slope_z, w_mid[layer_at - 1].T, preferred_element_type=jnp.float32
            ).astype(jnp.bfloat16)
        reduced = list(reduce_blocks(partial_in, waiting, 3 + layer_at))
        if layer_at > 0:
            upstream = reduced.pop(0)
            grads_mid.append(reduced.pop(0))
        else:
            grad_first = reduced.pop(0)
        if len(waiting) > 1:
            grad_out = reduced.pop(0)
        waiting = []
        grads_gain.append(gain_sum)
        grads_bias.append(bias_sum)
    grad_mid = jnp.stack(grads_mid[::-1])
    grad_gain = jnp.stack(grads_gain[::-1])
    grad_bias = jnp.stack(grads_bias[::-1])
    return (grad_first, grad_mid, grad_out, grad_gain, grad_bias)


def solution(mesh):
    return jax.shard_map(
        per_device,
        mesh=mesh,
        in_specs=(
            P("dp"),
            P(),
            P(),
            P(),
            P(),
            P(None, "mp"),
            P(None, None, "mp"),
            P("mp", None),
            P(None, "mp"),
            P(None, "mp"),
            P("dp", None),
        ),
        out_specs=(
            P("dp", "mp"),
            P(None, "dp", "mp"),
            P(("mp", "dp"), None),
            P(None, "mp"),
            P(None, "mp"),
        ),
        check_vma=False,
    )
```

```python
import functools
import math

import jax
import jax.numpy as jnp
from jax import lax
from jax.experimental import pallas as pl
from jax.experimental.pallas import tpu as pltpu
from jax.sharding import PartitionSpec as P

epsilon_norm = 1e-05


def encode(ids, hash_a, hash_b, hash_p, hash_m):
    p_real = hash_p.astype(jnp.float32)
    m_real = hash_m.astype(jnp.float32)
    p_inv, m_inv, scale = lax.optimization_barrier(
        (1.0 / p_real, 1.0 / m_real, 2.0 / (hash_m - 1).astype(jnp.float32))
    )
    ids_real = ids.astype(jnp.float32)
    guess = (ids_real[:, None] * p_inv[None, :]).astype(jnp.int32)
    reduced = ids[:, None] - guess * hash_p[None, :]
    mixed = hash_a[None, :] * reduced + hash_b[None, :]
    guess = jnp.floor(mixed.astype(jnp.float32) * p_inv[None, :]).astype(jnp.int32)
    rest = (mixed - guess * hash_p[None, :]).astype(jnp.float32)
    rest = jnp.where(rest < 0.0, rest + p_real[None, :], rest)
    rest = jnp.where(rest >= p_real[None, :], rest - p_real[None, :], rest)
    bucket = jnp.floor((rest + 0.5) * m_inv[None, :])
    hashed = rest - bucket * m_real[None, :]
    return (hashed * scale[None, :] - 1.0).astype(jnp.bfloat16)


def exchange_kernel(axis, n, x_ref, o_ref, held, send_sems, recv_sems):
    me = lax.axis_index(axis)
    barrier = pltpu.get_barrier_semaphore()
    for step in range(1, n):
        pl.semaphore_signal(
            barrier,
            inc=1,
            device_id={axis: lax.rem(me + step, n)},
            device_id_type=pl.DeviceIdType.MESH,
        )
    pl.semaphore_wait(barrier, n - 1)
    copies = []
    for step in range(1, n):
        copy = pltpu.make_async_remote_copy(
            src_ref=x_ref,
            dst_ref=held.at[me],
            send_sem=send_sems.at[step],
            recv_sem=recv_sems.at[step],
            device_id={axis: lax.rem(me + step, n)},
            device_id_type=pl.DeviceIdType.MESH,
        )
        copy.start()
        copies.append(copy)
    held[me] = x_ref[...]
    for copy in copies:
        copy.wait()
    total = held[0].astype(jnp.float32)
    for at in range(1, n):
        total = total + held[at].astype(jnp.float32)
    o_ref[...] = total


def exchange_sum(value, axis, collective, name):
    n = lax.axis_size(axis)
    return pl.pallas_call(
        functools.partial(exchange_kernel, axis, n),
        out_shape=jax.ShapeDtypeStruct(value.shape, jnp.float32),
        in_specs=[VMEM_SPEC],
        out_specs=VMEM_SPEC,
        scratch_shapes=[
            pltpu.VMEM((n,) + value.shape, value.dtype),
            pltpu.SemaphoreType.DMA((n,)),
            pltpu.SemaphoreType.DMA((n,)),
        ],
        compiler_params=pltpu.CompilerParams(
            collective_id=collective, has_side_effects=True, vmem_limit_bytes=4 << 20
        ),
        name=name,
    )(value)


def sum_pair(first, second, axis):
    total = exchange_sum(jnp.stack([first, second]).reshape(8, -1), axis, 0, "sum_pair")
    total = total.reshape(2, -1)
    return total[0], total[1]


VMEM_SPEC = pl.BlockSpec(memory_space=pltpu.VMEM)
MESH_ID = pl.DeviceIdType.MESH
CHUNKS = 4


def meet(targets):
    barrier = pltpu.get_barrier_semaphore()
    for target in targets:
        pl.semaphore_signal(barrier, inc=1, device_id=target, device_id_type=MESH_ID)
    pl.semaphore_wait(barrier, len(targets))


def quad_peers(axis):
    me = lax.axis_index(axis)
    near = me + 1 - 2 * lax.rem(me, 2)
    far = lax.rem(me + 2, 4)
    return me, near, far


def gather_kernel(axis, x_ref, o_ref, own_sem, send_sems, recv_sems):
    me, near, far = quad_peers(axis)
    rows, width = x_ref.shape
    part = rows // CHUNKS
    meet([{axis: near}, {axis: far}])

    def place(owner, at):
        return o_ref.at[pl.ds(at * part, part), pl.ds(pl.multiple_of(owner * width, 128), width)]

    def send(source, owner, at, slot, target):
        copy = pltpu.make_async_remote_copy(
            src_ref=source,
            dst_ref=place(owner, at),
            send_sem=send_sems.at[slot, at],
            recv_sem=recv_sems.at[slot, at],
            device_id={axis: target},
            device_id_type=MESH_ID,
        )
        copy.start()
        return copy

    own = []
    far_copies = []
    for at in range(CHUNKS):
        far_copies.append(send(x_ref.at[pl.ds(at * part, part)], me, at, 0, far))
    for at in range(CHUNKS):
        own.append(send(x_ref.at[pl.ds(at * part, part)], me, at, 1, near))
    local = pltpu.make_async_copy(
        x_ref, o_ref.at[:, pl.ds(pl.multiple_of(me * width, 128), width)], own_sem
    )
    local.start()
    for at in range(CHUNKS):
        far_copies[at].wait_recv()
        own.append(send(place(far, at), far, at, 2, near))
    for copy in far_copies:
        copy.wait_send()
    for copy in own:
        copy.wait()
    local.wait()


def gather_columns(value, axis):
    if lax.axis_size(axis) != 4:
        return lax.all_gather(value, axis, axis=1, tiled=True)
    rows, width = value.shape
    return pl.pallas_call(
        functools.partial(gather_kernel, axis),
        out_shape=jax.ShapeDtypeStruct((rows, 4 * width), value.dtype),
        in_specs=[VMEM_SPEC],
        out_specs=VMEM_SPEC,
        scratch_shapes=[
            pltpu.SemaphoreType.DMA,
            pltpu.SemaphoreType.DMA((3, CHUNKS)),
            pltpu.SemaphoreType.DMA((3, CHUNKS)),
        ],
        compiler_params=pltpu.CompilerParams(
            collective_id=2, has_side_effects=True, vmem_limit_bytes=16 << 20
        ),
        name="gather_columns",
    )(value)


def reduce_kernel(axis, n, quad, count, *refs):
    refs = list(refs)
    part_ref = refs.pop(0) if quad else None
    grads = [refs.pop(0) for _ in range(count)]
    up_ref = refs.pop(0) if quad else None
    outs = [refs.pop(0) for _ in range(count)]
    helds = [refs.pop(0) for _ in range(count)]
    pairs = [refs.pop(0) for _ in range(count)]
    sums = [refs.pop(0) for _ in range(count)]
    send_sems, recv_sems = refs.pop(0), refs.pop(0)
    rank = lax.axis_index(axis)
    half = n // 2
    beside = rank + 1 - 2 * lax.rem(rank, 2)
    turn = beside - rank
    peers = [lax.rem(rank + 2 * step, n) for step in range(1, half)]
    targets = [{axis: beside}] + [{axis: peer} for peer in peers]
    if quad:
        near_buf, sum_buf, far_buf, quad_send, quad_recv = refs
        me, near, far = quad_peers(quad)
        targets = targets + [{quad: near}, {quad: far}]
    meet(targets)
    if quad:
        rows = part_ref.shape[0]
        width = part_ref.shape[1] // 4
        part = rows // CHUNKS

        def columns(owner):
            return pl.ds(pl.multiple_of(owner * width, 128), width)

        near_copies = [[], []]
        for slot, owner in enumerate((lax.rem(near + 2, 4), near)):
            for at in range(CHUNKS):
                copy = pltpu.make_async_remote_copy(
                    src_ref=part_ref.at[pl.ds(at * part, part), columns(owner)],
                    dst_ref=near_buf.at[slot, pl.ds(at * part, part)],
                    send_sem=quad_send.at[slot, at],
                    recv_sem=quad_recv.at[slot, at],
                    device_id={quad: near},
                    device_id_type=MESH_ID,
                )
                copy.start()
                near_copies[slot].append(copy)
    pair_copies = []
    for which in range(count):
        block = outs[which].shape[0]
        copies = []
        for slot in [*range(1, half), 0]:
            owner = lax.rem(rank + 2 * slot, n) + turn
            copy = pltpu.make_async_remote_copy(
                src_ref=grads[which].at[pl.ds(pl.multiple_of(owner * block, 16), block)],
                dst_ref=pairs[which].at[slot],
                send_sem=send_sems.at[which, 0, slot],
                recv_sem=recv_sems.at[which, 0, slot],
                device_id={axis: beside},
                device_id_type=MESH_ID,
            )
            copy.start()
            copies.append(copy)
        pair_copies.append(copies)
    if quad:
        stride = 64
        far_copies = []
        for at in range(CHUNKS):
            near_copies[0][at].wait_recv()

            @pl.loop(0, part // stride)
            def _(line):
                here = pl.ds(pl.multiple_of(at * part + line * stride, 16), stride)
                sum_buf[here, :] = (
                    part_ref[here, columns(far)].astype(jnp.float32)
                    + near_buf[0, here, :].astype(jnp.float32)
                ).astype(sum_buf.dtype)

            copy = pltpu.make_async_remote_copy(
                src_ref=sum_buf.at[pl.ds(at * part, part)],
                dst_ref=far_buf.at[pl.ds(at * part, part)],
                send_sem=quad_send.at[2, at],
                recv_sem=quad_recv.at[2, at],
                device_id={quad: far},
                device_id_type=MESH_ID,
            )
            copy.start()
            far_copies.append(copy)

    grad_copies = []
    for which in range(count):
        block = outs[which].shape[0]
        stride = min(16, block)
        for step in range(1, half):
            pair_copies[which][step - 1].wait_recv()
            peer = peers[step - 1]

            @pl.loop(0, block // stride)
            def _(line):
                here = pl.ds(pl.multiple_of(line * stride, stride), stride)
                theirs = pl.ds(pl.multiple_of(peer * block + line * stride, stride), stride)
                sums[which][step - 1, here, :] = (
                    grads[which][theirs, :].astype(jnp.float32)
                    + pairs[which][step, here, :].astype(jnp.float32)
                ).astype(sums[which].dtype)

            copy = pltpu.make_async_remote_copy(
                src_ref=sums[which].at[step - 1],
                dst_ref=helds[which].at[step - 1],
                send_sem=send_sems.at[which, 1, step - 1],
                recv_sem=recv_sems.at[which, 1, step - 1],
                device_id={axis: peer},
                device_id_type=MESH_ID,
            )
            copy.start()
            grad_copies.append(copy)
    if quad:
        for at in range(CHUNKS):
            near_copies[1][at].wait_recv()
            far_copies[at].wait_recv()

            @pl.loop(0, part // stride)
            def _(line):
                here = pl.ds(pl.multiple_of(at * part + line * stride, 16), stride)
                up_ref[here, :] = (
                    part_ref[here, columns(me)].astype(jnp.float32)
                    + near_buf[1, here, :].astype(jnp.float32)
                    + far_buf[here, :].astype(jnp.float32)
                )

        for copy in near_copies[0] + near_copies[1] + far_copies:
            copy.wait_send()
    for which in range(count):
        pair_copies[which][half - 1].wait_recv()
        for copy in pair_copies[which]:
            copy.wait_send()
    for copy in grad_copies:
        copy.wait()
    for which in range(count):
        block = outs[which].shape[0]
        stride = min(16, block)

        @pl.loop(0, block // stride)
        def _(line):
            here = pl.ds(pl.multiple_of(line * stride, stride), stride)
            mine = pl.ds(pl.multiple_of(rank * block + line * stride, stride), stride)
            total = grads[which][mine, :].astype(jnp.float32)
            total = total + pairs[which][0, here, :].astype(jnp.float32)
            for step in range(half - 1):
                total = total + helds[which][step, here, :].astype(jnp.float32)
            outs[which][here, :] = total


def reduce_blocks(partial, grads, collective):
    n = lax.axis_size("dp")
    quad = "mp" if partial is not None else None
    count = len(grads)
    shapes = []
    scratch = []
    operands = []
    if quad:
        rows, width = partial.shape[0], partial.shape[1] // 4
        operands.append(partial)
        shapes.append(jax.ShapeDtypeStruct((rows, width), jnp.float32))
    for grad in grads:
        block = grad.shape[0] // n
        operands.append(grad)
        shapes.append(jax.ShapeDtypeStruct((block, grad.shape[1]), jnp.float32))
    half = n // 2
    for slots in (half - 1, half, half - 1):
        for grad in grads:
            scratch.append(pltpu.VMEM((slots, grad.shape[0] // n, grad.shape[1]), grad.dtype))
    scratch += [pltpu.SemaphoreType.DMA((count, 2, half))] * 2
    if quad:
        scratch += [
            pltpu.VMEM((2, rows, width), partial.dtype),
            pltpu.VMEM((rows, width), partial.dtype),
            pltpu.VMEM((rows, width), partial.dtype),
            pltpu.SemaphoreType.DMA((3, CHUNKS)),
            pltpu.SemaphoreType.DMA((3, CHUNKS)),
        ]
    return pl.pallas_call(
        functools.partial(reduce_kernel, "dp", n, quad, count),
        out_shape=shapes,
        in_specs=[VMEM_SPEC] * len(operands),
        out_specs=[VMEM_SPEC] * len(shapes),
        scratch_shapes=scratch,
        compiler_params=pltpu.CompilerParams(
            collective_id=collective, has_side_effects=True, vmem_limit_bytes=32 << 20
        ),
        name="reduce_blocks",
    )(*operands)


def mish_parts(values):
    small = jnp.exp(-jnp.abs(values))
    upper = values >= 0.0
    top = jnp.where(upper, 1.0 + 2.0 * small, small * (small + 2.0))
    rest = jnp.where(upper, 2.0 * small * small, 2.0)
    return small, upper, top, rest


def mish_act(values):
    _, _, top, rest = mish_parts(values)
    return values * (top / (top + rest))


def mish_slope(values):
    small, upper, top, rest = mish_parts(values)
    whole = top + rest
    inverse = 1.0 / (whole * (1.0 + small))
    each = inverse * (1.0 + small)
    tangent = top * each
    logistic = jnp.where(upper, 1.0, small) * (inverse * whole)
    return tangent + values * (rest * each) * (1.0 + tangent) * logistic


def column_stats(summed, batch_total):
    totals, squares = sum_pair(jnp.sum(summed, axis=0), jnp.sum(summed * summed, axis=0), "dp")
    average = totals / batch_total
    spread = squares / batch_total - average * average
    centered = summed - average
    inverse = 1.0 / jnp.sqrt(spread + epsilon_norm)
    return (centered * inverse, inverse)


def column_products(left_rows, right_rows):
    return jnp.dot(left_rows.T, right_rows, preferred_element_type=jnp.float32)


def per_device(ids, hash_a, hash_b, hash_p, hash_m, w_in, w_mid, w_out, bn_gain, bn_bias, target):
    batch_devices = lax.axis_size("dp")
    batch_total = ids.shape[0] * batch_devices
    layer_count = bn_gain.shape[0]
    encoded = lax.optimization_barrier(encode(ids, hash_a, hash_b, hash_p, hash_m))
    full_inputs = []
    saved = []
    current = encoded
    for layer_at in range(layer_count):
        if layer_at == 0:
            whole_input = encoded
            summed = jnp.dot(whole_input, w_in, preferred_element_type=jnp.float32)
        else:
            whole_input = gather_columns(current, "mp")
            summed = jnp.dot(whole_input, w_mid[layer_at - 1], preferred_element_type=jnp.float32)
        full_inputs.append(whole_input)
        normed, inverse = column_stats(summed, batch_total)
        shifted = bn_gain[layer_at] * normed + bn_bias[layer_at]
        current = mish_act(shifted).astype(jnp.bfloat16)
        saved.append((normed, inverse, shifted))
    partial_out = jnp.dot(current, w_out, preferred_element_type=jnp.float32).T
    predicted = exchange_sum(partial_out.astype(jnp.bfloat16), "mp", 1, "sum_output").T
    residual_out = ((predicted - target) / math.sqrt(batch_total)).astype(jnp.bfloat16)
    waiting = [column_products(current, residual_out).astype(jnp.bfloat16)]
    grad_out = None
    upstream = jnp.dot(residual_out, w_out.T, preferred_element_type=jnp.float32)
    grads_gain = []
    grads_bias = []
    grads_mid = []
    grad_first = None
    for layer_at in reversed(range(layer_count)):
        normed, inverse, shifted = saved[layer_at]
        slope_a = upstream * mish_slope(shifted)
        bias_sum, gain_sum = sum_pair(
            jnp.sum(slope_a, axis=0), jnp.sum(slope_a * normed, axis=0), "dp"
        )
        slope_z = (
            bn_gain[layer_at]
            * inverse
            * (slope_a - bias_sum / batch_total - normed * gain_sum / batch_total)
        ).astype(jnp.bfloat16)
        whole_input = full_inputs[layer_at]
        waiting = [column_products(whole_input, slope_z).astype(jnp.bfloat16)] + waiting
        partial_in = None
        if layer_at > 0:
            partial_in = jnp.dot(
                slope_z, w_mid[layer_at - 1].T, preferred_element_type=jnp.float32
            ).astype(jnp.bfloat16)
        reduced = list(reduce_blocks(partial_in, waiting, 3 + layer_at))
        if layer_at > 0:
            upstream = reduced.pop(0)
            grads_mid.append(reduced.pop(0))
        else:
            grad_first = reduced.pop(0)
        if len(waiting) > 1:
            grad_out = reduced.pop(0)
        waiting = []
        grads_gain.append(gain_sum)
        grads_bias.append(bias_sum)
    grad_mid = jnp.stack(grads_mid[::-1])
    grad_gain = jnp.stack(grads_gain[::-1])
    grad_bias = jnp.stack(grads_bias[::-1])
    return (grad_first, grad_mid, grad_out, grad_gain, grad_bias)


def solution(mesh):
    return jax.shard_map(
        per_device,
        mesh=mesh,
        in_specs=(
            P("dp"),
            P(),
            P(),
            P(),
            P(),
            P(None, "mp"),
            P(None, None, "mp"),
            P("mp", None),
            P(None, "mp"),
            P(None, "mp"),
            P("dp", None),
        ),
        out_specs=(
            P("dp", "mp"),
            P(None, "dp", "mp"),
            P(("mp", "dp"), None),
            P(None, "mp"),
            P(None, "mp"),
        ),
        check_vma=False,
    )
```

```python
import functools
import math

import jax
import jax.numpy as jnp
from jax import lax
from jax.experimental import pallas as pl
from jax.experimental.pallas import tpu as pltpu
from jax.sharding import PartitionSpec as P

epsilon_norm = 1e-05


def encode(ids, hash_a, hash_b, hash_p, hash_m):
    p_real = hash_p.astype(jnp.float32)
    m_real = hash_m.astype(jnp.float32)
    p_inv, m_inv, scale = lax.optimization_barrier(
        (1.0 / p_real, 1.0 / m_real, 2.0 / (hash_m - 1).astype(jnp.float32))
    )
    ids_real = ids.astype(jnp.float32)
    guess = (ids_real[:, None] * p_inv[None, :]).astype(jnp.int32)
    reduced = ids[:, None] - guess * hash_p[None, :]
    mixed = hash_a[None, :] * reduced + hash_b[None, :]
    guess = jnp.floor(mixed.astype(jnp.float32) * p_inv[None, :]).astype(jnp.int32)
    rest = (mixed - guess * hash_p[None, :]).astype(jnp.float32)
    rest = jnp.where(rest < 0.0, rest + p_real[None, :], rest)
    rest = jnp.where(rest >= p_real[None, :], rest - p_real[None, :], rest)
    bucket = jnp.floor((rest + 0.5) * m_inv[None, :])
    hashed = rest - bucket * m_real[None, :]
    return (hashed * scale[None, :] - 1.0).astype(jnp.bfloat16)


def exchange_kernel(axis, n, x_ref, o_ref, held, send_sems, recv_sems):
    me = lax.axis_index(axis)
    barrier = pltpu.get_barrier_semaphore()
    for step in range(1, n):
        pl.semaphore_signal(
            barrier,
            inc=1,
            device_id={axis: lax.rem(me + step, n)},
            device_id_type=pl.DeviceIdType.MESH,
        )
    pl.semaphore_wait(barrier, n - 1)
    copies = []
    for step in range(1, n):
        copy = pltpu.make_async_remote_copy(
            src_ref=x_ref,
            dst_ref=held.at[me],
            send_sem=send_sems.at[step],
            recv_sem=recv_sems.at[step],
            device_id={axis: lax.rem(me + step, n)},
            device_id_type=pl.DeviceIdType.MESH,
        )
        copy.start()
        copies.append(copy)
    held[me] = x_ref[...]
    for copy in copies:
        copy.wait()
    total = held[0].astype(jnp.float32)
    for at in range(1, n):
        total = total + held[at].astype(jnp.float32)
    o_ref[...] = total


def exchange_sum(value, axis, collective, name):
    n = lax.axis_size(axis)
    return pl.pallas_call(
        functools.partial(exchange_kernel, axis, n),
        out_shape=jax.ShapeDtypeStruct(value.shape, jnp.float32),
        in_specs=[VMEM_SPEC],
        out_specs=VMEM_SPEC,
        scratch_shapes=[
            pltpu.VMEM((n,) + value.shape, value.dtype),
            pltpu.SemaphoreType.DMA((n,)),
            pltpu.SemaphoreType.DMA((n,)),
        ],
        compiler_params=pltpu.CompilerParams(
            collective_id=collective, has_side_effects=True, vmem_limit_bytes=4 << 20
        ),
        name=name,
    )(value)


def sum_pair(first, second, axis):
    total = exchange_sum(jnp.stack([first, second]).reshape(8, -1), axis, 0, "sum_pair")
    total = total.reshape(2, -1)
    return total[0], total[1]


VMEM_SPEC = pl.BlockSpec(memory_space=pltpu.VMEM)
MESH_ID = pl.DeviceIdType.MESH
CHUNKS = 8


def meet(targets):
    barrier = pltpu.get_barrier_semaphore()
    for target in targets:
        pl.semaphore_signal(barrier, inc=1, device_id=target, device_id_type=MESH_ID)
    pl.semaphore_wait(barrier, len(targets))


def quad_peers(axis):
    me = lax.axis_index(axis)
    near = me + 1 - 2 * lax.rem(me, 2)
    far = lax.rem(me + 2, 4)
    return me, near, far


def gather_kernel(axis, x_ref, o_ref, own_sem, send_sems, recv_sems):
    me, near, far = quad_peers(axis)
    rows, width = x_ref.shape
    part = rows // CHUNKS
    meet([{axis: near}, {axis: far}])

    def place(owner, at):
        return o_ref.at[pl.ds(at * part, part), pl.ds(pl.multiple_of(owner * width, 128), width)]

    def send(source, owner, at, slot, target):
        copy = pltpu.make_async_remote_copy(
            src_ref=source,
            dst_ref=place(owner, at),
            send_sem=send_sems.at[slot, at],
            recv_sem=recv_sems.at[slot, at],
            device_id={axis: target},
            device_id_type=MESH_ID,
        )
        copy.start()
        return copy

    own = []
    far_copies = []
    for at in range(CHUNKS):
        far_copies.append(send(x_ref.at[pl.ds(at * part, part)], me, at, 0, far))
    for at in range(CHUNKS):
        own.append(send(x_ref.at[pl.ds(at * part, part)], me, at, 1, near))
    local = pltpu.make_async_copy(
        x_ref, o_ref.at[:, pl.ds(pl.multiple_of(me * width, 128), width)], own_sem
    )
    local.start()
    for at in range(CHUNKS):
        far_copies[at].wait_recv()
        own.append(send(place(far, at), far, at, 2, near))
    for copy in far_copies:
        copy.wait_send()
    for copy in own:
        copy.wait()
    local.wait()


def gather_columns(value, axis):
    if lax.axis_size(axis) != 4:
        return lax.all_gather(value, axis, axis=1, tiled=True)
    rows, width = value.shape
    return pl.pallas_call(
        functools.partial(gather_kernel, axis),
        out_shape=jax.ShapeDtypeStruct((rows, 4 * width), value.dtype),
        in_specs=[VMEM_SPEC],
        out_specs=VMEM_SPEC,
        scratch_shapes=[
            pltpu.SemaphoreType.DMA,
            pltpu.SemaphoreType.DMA((3, CHUNKS)),
            pltpu.SemaphoreType.DMA((3, CHUNKS)),
        ],
        compiler_params=pltpu.CompilerParams(
            collective_id=2, has_side_effects=True, vmem_limit_bytes=16 << 20
        ),
        name="gather_columns",
    )(value)


def reduce_kernel(axis, n, quad, count, *refs):
    refs = list(refs)
    part_ref = refs.pop(0) if quad else None
    grads = [refs.pop(0) for _ in range(count)]
    up_ref = refs.pop(0) if quad else None
    outs = [refs.pop(0) for _ in range(count)]
    helds = [refs.pop(0) for _ in range(count)]
    pairs = [refs.pop(0) for _ in range(count)]
    sums = [refs.pop(0) for _ in range(count)]
    send_sems, recv_sems = refs.pop(0), refs.pop(0)
    rank = lax.axis_index(axis)
    half = n // 2
    beside = rank + 1 - 2 * lax.rem(rank, 2)
    turn = beside - rank
    peers = [lax.rem(rank + 2 * step, n) for step in range(1, half)]
    targets = [{axis: beside}] + [{axis: peer} for peer in peers]
    if quad:
        near_buf, sum_buf, far_buf, quad_send, quad_recv = refs
        me, near, far = quad_peers(quad)
        targets = targets + [{quad: near}, {quad: far}]
    meet(targets)
    if quad:
        rows = part_ref.shape[0]
        width = part_ref.shape[1] // 4
        part = rows // CHUNKS

        def columns(owner):
            return pl.ds(pl.multiple_of(owner * width, 128), width)

        near_copies = [[], []]
        for slot, owner in enumerate((lax.rem(near + 2, 4), near)):
            for at in range(CHUNKS):
                copy = pltpu.make_async_remote_copy(
                    src_ref=part_ref.at[pl.ds(at * part, part), columns(owner)],
                    dst_ref=near_buf.at[slot, pl.ds(at * part, part)],
                    send_sem=quad_send.at[slot, at],
                    recv_sem=quad_recv.at[slot, at],
                    device_id={quad: near},
                    device_id_type=MESH_ID,
                )
                copy.start()
                near_copies[slot].append(copy)
    pair_copies = []
    for which in range(count):
        block = outs[which].shape[0]
        copies = []
        for slot in [*range(1, half), 0]:
            owner = lax.rem(rank + 2 * slot, n) + turn
            copy = pltpu.make_async_remote_copy(
                src_ref=grads[which].at[pl.ds(pl.multiple_of(owner * block, 16), block)],
                dst_ref=pairs[which].at[slot],
                send_sem=send_sems.at[which, 0, slot],
                recv_sem=recv_sems.at[which, 0, slot],
                device_id={axis: beside},
                device_id_type=MESH_ID,
            )
            copy.start()
            copies.append(copy)
        pair_copies.append(copies)
    if quad:
        stride = 64
        far_copies = []
        for at in range(CHUNKS):
            near_copies[0][at].wait_recv()

            @pl.loop(0, part // stride)
            def _(line):
                here = pl.ds(pl.multiple_of(at * part + line * stride, 16), stride)
                sum_buf[here, :] = (
                    part_ref[here, columns(far)].astype(jnp.float32)
                    + near_buf[0, here, :].astype(jnp.float32)
                ).astype(sum_buf.dtype)

            copy = pltpu.make_async_remote_copy(
                src_ref=sum_buf.at[pl.ds(at * part, part)],
                dst_ref=far_buf.at[pl.ds(at * part, part)],
                send_sem=quad_send.at[2, at],
                recv_sem=quad_recv.at[2, at],
                device_id={quad: far},
                device_id_type=MESH_ID,
            )
            copy.start()
            far_copies.append(copy)

    grad_copies = []
    for which in range(count):
        block = outs[which].shape[0]
        stride = min(16, block)
        for step in range(1, half):
            pair_copies[which][step - 1].wait_recv()
            peer = peers[step - 1]

            @pl.loop(0, block // stride)
            def _(line):
                here = pl.ds(pl.multiple_of(line * stride, stride), stride)
                theirs = pl.ds(pl.multiple_of(peer * block + line * stride, stride), stride)
                sums[which][step - 1, here, :] = (
                    grads[which][theirs, :].astype(jnp.float32)
                    + pairs[which][step, here, :].astype(jnp.float32)
                ).astype(sums[which].dtype)

            copy = pltpu.make_async_remote_copy(
                src_ref=sums[which].at[step - 1],
                dst_ref=helds[which].at[step - 1],
                send_sem=send_sems.at[which, 1, step - 1],
                recv_sem=recv_sems.at[which, 1, step - 1],
                device_id={axis: peer},
                device_id_type=MESH_ID,
            )
            copy.start()
            grad_copies.append(copy)
    if quad:
        for at in range(CHUNKS):
            near_copies[1][at].wait_recv()
            far_copies[at].wait_recv()

            @pl.loop(0, part // stride)
            def _(line):
                here = pl.ds(pl.multiple_of(at * part + line * stride, 16), stride)
                up_ref[here, :] = (
                    part_ref[here, columns(me)].astype(jnp.float32)
                    + near_buf[1, here, :].astype(jnp.float32)
                    + far_buf[here, :].astype(jnp.float32)
                )

        for copy in near_copies[0] + near_copies[1] + far_copies:
            copy.wait_send()
    for which in range(count):
        pair_copies[which][half - 1].wait_recv()
        for copy in pair_copies[which]:
            copy.wait_send()
    for copy in grad_copies:
        copy.wait()
    for which in range(count):
        block = outs[which].shape[0]
        stride = min(16, block)

        @pl.loop(0, block // stride)
        def _(line):
            here = pl.ds(pl.multiple_of(line * stride, stride), stride)
            mine = pl.ds(pl.multiple_of(rank * block + line * stride, stride), stride)
            total = grads[which][mine, :].astype(jnp.float32)
            total = total + pairs[which][0, here, :].astype(jnp.float32)
            for step in range(half - 1):
                total = total + helds[which][step, here, :].astype(jnp.float32)
            outs[which][here, :] = total


def reduce_blocks(partial, grads, collective):
    n = lax.axis_size("dp")
    quad = "mp" if partial is not None else None
    count = len(grads)
    shapes = []
    scratch = []
    operands = []
    if quad:
        rows, width = partial.shape[0], partial.shape[1] // 4
        operands.append(partial)
        shapes.append(jax.ShapeDtypeStruct((rows, width), jnp.float32))
    for grad in grads:
        block = grad.shape[0] // n
        operands.append(grad)
        shapes.append(jax.ShapeDtypeStruct((block, grad.shape[1]), jnp.float32))
    half = n // 2
    for slots in (half - 1, half, half - 1):
        for grad in grads:
            scratch.append(pltpu.VMEM((slots, grad.shape[0] // n, grad.shape[1]), grad.dtype))
    scratch += [pltpu.SemaphoreType.DMA((count, 2, half))] * 2
    if quad:
        scratch += [
            pltpu.VMEM((2, rows, width), partial.dtype),
            pltpu.VMEM((rows, width), partial.dtype),
            pltpu.VMEM((rows, width), partial.dtype),
            pltpu.SemaphoreType.DMA((3, CHUNKS)),
            pltpu.SemaphoreType.DMA((3, CHUNKS)),
        ]
    return pl.pallas_call(
        functools.partial(reduce_kernel, "dp", n, quad, count),
        out_shape=shapes,
        in_specs=[VMEM_SPEC] * len(operands),
        out_specs=[VMEM_SPEC] * len(shapes),
        scratch_shapes=scratch,
        compiler_params=pltpu.CompilerParams(
            collective_id=collective, has_side_effects=True, vmem_limit_bytes=32 << 20
        ),
        name="reduce_blocks",
    )(*operands)


def mish_parts(values):
    small = jnp.exp(-jnp.abs(values))
    upper = values >= 0.0
    top = jnp.where(upper, 1.0 + 2.0 * small, small * (small + 2.0))
    rest = jnp.where(upper, 2.0 * small * small, 2.0)
    return small, upper, top, rest


def mish_act(values):
    _, _, top, rest = mish_parts(values)
    return values * (top / (top + rest))


def mish_slope(values):
    small, upper, top, rest = mish_parts(values)
    whole = top + rest
    inverse = 1.0 / (whole * (1.0 + small))
    each = inverse * (1.0 + small)
    tangent = top * each
    logistic = jnp.where(upper, 1.0, small) * (inverse * whole)
    return tangent + values * (rest * each) * (1.0 + tangent) * logistic


def column_stats(summed, batch_total):
    totals, squares = sum_pair(jnp.sum(summed, axis=0), jnp.sum(summed * summed, axis=0), "dp")
    average = totals / batch_total
    spread = squares / batch_total - average * average
    centered = summed - average
    inverse = 1.0 / jnp.sqrt(spread + epsilon_norm)
    return (centered * inverse, inverse)


def column_products(left_rows, right_rows):
    return jnp.dot(left_rows.T, right_rows, preferred_element_type=jnp.float32)


def per_device(ids, hash_a, hash_b, hash_p, hash_m, w_in, w_mid, w_out, bn_gain, bn_bias, target):
    batch_devices = lax.axis_size("dp")
    batch_total = ids.shape[0] * batch_devices
    layer_count = bn_gain.shape[0]
    encoded = lax.optimization_barrier(encode(ids, hash_a, hash_b, hash_p, hash_m))
    full_inputs = []
    saved = []
    current = encoded
    for layer_at in range(layer_count):
        if layer_at == 0:
            whole_input = encoded
            summed = jnp.dot(whole_input, w_in, preferred_element_type=jnp.float32)
        else:
            whole_input = gather_columns(current, "mp")
            summed = jnp.dot(whole_input, w_mid[layer_at - 1], preferred_element_type=jnp.float32)
        full_inputs.append(whole_input)
        normed, inverse = column_stats(summed, batch_total)
        shifted = bn_gain[layer_at] * normed + bn_bias[layer_at]
        current = mish_act(shifted).astype(jnp.bfloat16)
        saved.append((normed, inverse, shifted))
    partial_out = jnp.dot(current, w_out, preferred_element_type=jnp.float32).T
    predicted = exchange_sum(partial_out.astype(jnp.bfloat16), "mp", 1, "sum_output").T
    residual_out = ((predicted - target) / math.sqrt(batch_total)).astype(jnp.bfloat16)
    waiting = [column_products(current, residual_out).astype(jnp.bfloat16)]
    grad_out = None
    upstream = jnp.dot(residual_out, w_out.T, preferred_element_type=jnp.float32)
    grads_gain = []
    grads_bias = []
    grads_mid = []
    grad_first = None
    for layer_at in reversed(range(layer_count)):
        normed, inverse, shifted = saved[layer_at]
        slope_a = upstream * mish_slope(shifted)
        bias_sum, gain_sum = sum_pair(
            jnp.sum(slope_a, axis=0), jnp.sum(slope_a * normed, axis=0), "dp"
        )
        slope_z = (
            bn_gain[layer_at]
            * inverse
            * (slope_a - bias_sum / batch_total - normed * gain_sum / batch_total)
        ).astype(jnp.bfloat16)
        whole_input = full_inputs[layer_at]
        waiting = [column_products(whole_input, slope_z).astype(jnp.bfloat16)] + waiting
        partial_in = None
        if layer_at > 0:
            partial_in = jnp.dot(
                slope_z, w_mid[layer_at - 1].T, preferred_element_type=jnp.float32
            ).astype(jnp.bfloat16)
        reduced = list(reduce_blocks(partial_in, waiting, 3 + layer_at))
        if layer_at > 0:
            upstream = reduced.pop(0)
            grads_mid.append(reduced.pop(0))
        else:
            grad_first = reduced.pop(0)
        if len(waiting) > 1:
            grad_out = reduced.pop(0)
        waiting = []
        grads_gain.append(gain_sum)
        grads_bias.append(bias_sum)
    grad_mid = jnp.stack(grads_mid[::-1])
    grad_gain = jnp.stack(grads_gain[::-1])
    grad_bias = jnp.stack(grads_bias[::-1])
    return (grad_first, grad_mid, grad_out, grad_gain, grad_bias)


def solution(mesh):
    return jax.shard_map(
        per_device,
        mesh=mesh,
        in_specs=(
            P("dp"),
            P(),
            P(),
            P(),
            P(),
            P(None, "mp"),
            P(None, None, "mp"),
            P("mp", None),
            P(None, "mp"),
            P(None, "mp"),
            P("dp", None),
        ),
        out_specs=(
            P("dp", "mp"),
            P(None, "dp", "mp"),
            P(("mp", "dp"), None),
            P(None, "mp"),
            P(None, "mp"),
        ),
        check_vma=False,
    )
```
